32 devices in a mesh: zone: 8 (over z, core), line: 4 (over y, x).
Axes of the slice: x: 2, y: 2, z: 4, core: 2. Of those that a mesh axis runs over, the one named last changes fastest.
Arguments:
- flow_state: float32 [8, 5, 64, 128, 128], P('zone', None, 'line'), may hold values from -6 to 6
- derivative: float32 [2, 128, 128], replicated, may hold values from -0.5 to 0.5
- derivative_z: float32 [64, 64], replicated, may hold values from -0.75 to 0.75
- line_inverse: float32 [8, 2, 5, 128, 128], P('zone')
- line_inverse_z: float32 [8, 5, 64, 64], P('zone')
- mixers: float32 [8, 7, 5, 5], P('zone')
- zone_size: int32 [8], P('zone'), may hold values from 1 to 64, 170 in all
- receiver_line: int32 [8, 4, 128], P('zone', 'line'), may hold values from 0 to 2047, as said below
- donor_group: int32 [8, 4, 128, 1], P('zone', 'line'), may hold values from 0 to 7; in each aligned block of 128 rows (0 to 127, 128 to 255, ..., all dimensions but the last counted through in order) at most 40 rows name the same one
- donor_line: int32 [8, 4, 128, 2], P('zone', 'line'), may hold values from 0 to 2047
- stencil_weight: float32 [8, 4, 128], P('zone', 'line'), may hold values from 0 to 1
Outputs:
- state_update: float32 [8, 5, 64, 128, 128], P('zone', None, 'line')
The draws below stay inside these ranges and needn't reach their ends.
Inputs may be any that keep to these rules, and one draw needn't show every extreme that they name: `receiver_line`: within one line block of one group the 128 receiver lines are distinct. `donor_group`: among the 128 slots of one line block of one group no donor group is named more than 40 times; in some line blocks some donor group is named exactly 40 times. `zone_size`: the sizes of all groups add up to 170, and the largest is 64.
All inputs are finite; a program needn't handle non-finite values.
Results may differ from the reference program's by a relative error of at most 0.0003.
Values sent between devices are 32-bit elements; how exact they have to be, the bound alone decides.
No kernel may reach another device: no remote copies, remote signals or barrier semaphores. Data moves between devices by JAX's collectives and lax.ppermute only.
A program may use at most 128 MiB of HBM per device.

```python
import math
import jax
import jax.numpy as jnp
import numpy as np
from jax import lax

EDGE_CELLS = 128
ZCELLS = 64
RECEIVERS = 128
GROUPS = 8
BLOCKS = 4
BLOCK_LINES = 2048
CAPACITY = 40


def draw_line_inverse(key, part):
    shape = (GROUPS, 2, 5, EDGE_CELLS, EDGE_CELLS)
    noise = jax.random.normal(key, shape, jnp.float32)
    return 0.8 * jnp.eye(EDGE_CELLS, dtype=jnp.float32) + 0.4 / math.sqrt(EDGE_CELLS) * noise


def draw_line_inverse_z(key, part):
    shape = (GROUPS, 5, ZCELLS, ZCELLS)
    noise = jax.random.normal(key, shape, jnp.float32)
    return 0.8 * jnp.eye(ZCELLS, dtype=jnp.float32) + 0.4 / math.sqrt(ZCELLS) * noise


def draw_mixers(key, part):
    noise = jax.random.normal(key, (GROUPS, 7, 5, 5), jnp.float32)
    return 0.8 * jnp.eye(5, dtype=jnp.float32) + 0.15 * noise


def draw_receiver_line(key, part):
    keys = jax.random.split(key, GROUPS * BLOCKS)
    chosen = jax.vmap(lambda single: jax.random.permutation(single, BLOCK_LINES)[:RECEIVERS])(keys)
    return chosen.reshape(GROUPS, BLOCKS, RECEIVERS).astype(jnp.int32)


def touch_ends(values, stream_key, low, high):
    extent = values.shape
    place = [jax.random.randint(jax.random.fold_in(stream_key, axis), (), 0, extent[axis]) for axis in range(len(extent))]
    values = values.at[tuple(place)].set(low)
    longest = extent.index(max(extent))
    place[longest] = (place[longest] + 1) % extent[longest]
    return values.at[tuple(place)].set(high)


def block_scale(own_key, shape, shards, smallest, largest):
    loudness, own = 1.0, jax.random.fold_in(own_key, 6)
    for position, parts in shards:
        draws = jnp.exp(jax.random.uniform(jax.random.fold_in(own, position), (parts,), jnp.float32, smallest / len(shards), largest / len(shards)))
        loudness = loudness * jnp.repeat(draws, shape[position] // parts).reshape([-1 if axis == position else 1 for axis in range(len(shape))])
    return loudness


def length_profile(number_of, total, bound, skew):
    portions = [(1 << 20) // math.isqrt(rank ** skew) + 1 for rank in range(2, number_of + 1)]
    rest, holding = total - bound - (number_of - 1), [1] * (number_of - 1)
    while rest > 0:
        candidates = [i for i in range(number_of - 1) if holding[i] < bound]
        whole, budget = sum([portions[i] for i in candidates]), rest
        for i in candidates:
            extra = min(bound - holding[i], max(1, budget * portions[i] // whole), rest)
            holding[i] = holding[i] + extra
            rest = rest - extra
    return np.array([bound] + holding)


def ragged_sizes(key, count, total, limit, skew):
    if count == 2:
        one = jax.random.randint(key, (), max(1, total - limit), min(limit, total - 1) + 1)
        return jnp.stack([one, total - one])
    tallies = jnp.asarray(length_profile(count, total, limit, skew), jnp.int32)
    pairs = (count - 1) // 2
    giver, receiver = tallies[1:1 + 2 * pairs:2], tallies[2:2 + 2 * pairs:2]
    room = jnp.minimum(giver - 1, limit - receiver)
    shifted = jax.random.randint(jax.random.fold_in(key, 1), (pairs,), 0, 1 << 20) % (room + 1)
    tallies = tallies.at[1:1 + 2 * pairs:2].set(giver - shifted).at[2:2 + 2 * pairs:2].set(receiver + shifted)
    return tallies[jax.random.permutation(jax.random.fold_in(key, 2), count)]


def routed_block(key, own, number, rows, amount, top, reach, slope):
    order = jax.random.permutation(key, amount)
    heavy_load, ordinary = load_shares(amount, rows * top, reach, slope, True), load_shares(amount, rows * top, reach, slope, False)
    places = jnp.arange(amount)

    def named(lengths, rotation):
        used = int((lengths > 0).sum())
        fixed = max(1, used // 4)
        passed = fixed + (places - fixed + rotation * (used - fixed)) % max(1, amount - fixed)
        return jnp.zeros((amount,), jnp.int32).at[order[jnp.where(places < fixed, places, passed)]].set(jnp.asarray(lengths, jnp.int32))

    lengths = jnp.where(number % 4 == 0, named(heavy_load, number // 4), named(ordinary, number - number // 4 - 1))
    mixed = jax.random.permutation(jax.random.fold_in(own, 3), amount)
    source_of, sink = mixed[0:amount // 2 * 2:2], mixed[1:amount // 2 * 2:2]
    slack = jnp.minimum(lengths[source_of] - 1, reach - lengths[sink]) // 2
    slack = jnp.where((source_of == order[0]) | (sink == order[0]) | (lengths[sink] == 0), 0, jnp.maximum(slack, 0))
    passed = jax.random.randint(jax.random.fold_in(own, 4), (amount // 2,), 0, 1 << 20) % (slack + 1)
    lengths = lengths.at[source_of].add(-passed).at[sink].add(passed)
    labels = jnp.searchsorted(jnp.cumsum(lengths), jnp.arange(rows * top), side="right").astype(jnp.int32)
    listing = labels.reshape(top, rows).T
    listing = listing[jax.random.permutation(jax.random.fold_in(own, 1), rows)]
    rotation = jax.random.randint(jax.random.fold_in(own, 2), (rows, 1), 0, top)
    return jnp.take_along_axis(listing, (jnp.arange(top)[None, :] + rotation) % top, axis=1)


def load_shares(number_of, total, bound, slope, full):
    portions = [(1 << 20) // math.isqrt(rank ** slope) + 1 for rank in range(1, number_of + 1)]
    largest = bound if full else min(bound, max(-(-total // number_of), total * portions[0] // sum(portions)))
    least = 1 if total - largest >= number_of - 1 else 0
    given, surplus = [largest] + [least] * (number_of - 1), total - largest - least * (number_of - 1)
    while surplus > 0:
        free = [i for i in range(1, number_of) if given[i] < largest] or [i for i in range(1, number_of) if given[i] < bound]
        pool, budget = sum([portions[i] for i in free]), surplus
        for i in free:
            addition = min(bound - given[i], max(1, budget * portions[i] // pool), surplus)
            given[i] = given[i] + addition
            surplus = surplus - addition
    return np.array(given)


def scatter_about(own_key, shape, scale, reach, pieces=(), kind=jnp.bfloat16):
    entries = jax.random.normal(own_key, shape, jnp.float32) * scale
    if len(pieces) > 0:
        entries = block_scale(own_key, shape, pieces, -0.22, 0.18) * entries
    return jnp.clip(entries, min=-reach, max=reach).astype(kind)


def setup_inputs(seed: int = 0) -> dict:
    key_of = jax.random.split(jax.random.key(seed), 12)
    flow_state = scatter_about(key_of[0], (GROUPS, 5, ZCELLS, EDGE_CELLS, EDGE_CELLS), 1.0, 6.0, ((0, 8), (2, 4)), jnp.float32)
    derivative = scatter_about(key_of[1], (2, EDGE_CELLS, EDGE_CELLS), EDGE_CELLS ** -0.5, 0.5, (), jnp.float32)
    derivative_z = scatter_about(key_of[2], (ZCELLS, ZCELLS), ZCELLS ** -0.5, 0.75, (), jnp.float32)
    line_inverse = draw_line_inverse(jax.random.fold_in(key_of[11], 71), 0)
    line_inverse_z = draw_line_inverse_z(jax.random.fold_in(key_of[11], 71), 0)
    mixers = draw_mixers(jax.random.fold_in(key_of[11], 71), 0)
    zone_size = ragged_sizes(key_of[6], GROUPS, GROUPS * ZCELLS // 3, ZCELLS, 2).astype(jnp.int32)
    receiver_line = draw_receiver_line(jax.random.fold_in(key_of[11], 71), 0)
    donor_group_keys = jax.random.split(jax.random.fold_in(key_of[8], 1), GROUPS * BLOCKS * RECEIVERS // RECEIVERS)
    donor_group_turns = jax.random.permutation(jax.random.fold_in(key_of[8], 3), GROUPS * BLOCKS * RECEIVERS // RECEIVERS)
    donor_group = jax.vmap(lambda own, number: routed_block(jax.random.fold_in(key_of[8], 2), own, number, RECEIVERS, GROUPS, 1, CAPACITY, 2))(donor_group_keys, donor_group_turns).reshape((GROUPS, BLOCKS, RECEIVERS, 1))
    donor_line = touch_ends(jax.random.randint(key_of[9], (GROUPS, BLOCKS, RECEIVERS, 2), 0, BLOCK_LINES), jax.random.fold_in(key_of[9], 1), 0, BLOCK_LINES - 1).astype(jnp.int32)
    stencil_weight = jnp.clip(1.0 * jax.random.uniform(key_of[10], (GROUPS, BLOCKS, RECEIVERS), jnp.float32) ** block_scale(key_of[10], (GROUPS, BLOCKS, RECEIVERS), ((0, 8), (1, 4)), -0.2, 0.2), 0.0, 1.0)
    return {"flow_state": flow_state, "derivative": derivative, "derivative_z": derivative_z, "line_inverse": line_inverse, "line_inverse_z": line_inverse_z, "mixers": mixers, "zone_size": zone_size, "receiver_line": receiver_line, "donor_group": donor_group, "donor_line": donor_line, "stencil_weight": stencil_weight}


highest = lax.Precision.HIGHEST


def apply_mixer(matrix, fields):
    return jnp.einsum('mv,vkji->mkji', matrix, fields, precision=highest)


def reference(flow_state, derivative, derivative_z, line_inverse, line_inverse_z, mixers, zone_size, receiver_line, donor_group, donor_line, stencil_weight):
    line_view = flow_state.reshape(GROUPS, 5, BLOCKS, BLOCK_LINES, EDGE_CELLS)
    block_index = jnp.arange(BLOCKS, dtype=jnp.int32)[:, None]

    def one_group(group):
        fields = flow_state[group]
        mixing = mixers[group]
        inverses = line_inverse[group]
        inverse_z = line_inverse_z[group]
        term_x = jnp.einsum('vkji,mi->vkjm', apply_mixer(mixing[0], fields), derivative[0], precision=highest)
        term_y = jnp.einsum('vkji,mj->vkmi', apply_mixer(mixing[1], fields), derivative[1], precision=highest)
        term_z = jnp.einsum('vkji,mk->vmji', apply_mixer(mixing[2], fields), derivative_z, precision=highest)
        active = jnp.arange(ZCELLS, dtype=jnp.int32) < zone_size[group]
        residual = jnp.where(active[None, :, None, None], -(term_x + term_y + term_z), 0.0)
        donors = donor_group[group][:, :, 0]
        first_rows = line_view[donors, :, block_index, donor_line[group][:, :, 0]]
        second_rows = line_view[donors, :, block_index, donor_line[group][:, :, 1]]
        weight = stencil_weight[group][:, :, None, None]
        interp = weight * first_rows + (1.0 - weight) * second_rows
        receivers = receiver_line[group]
        own_rows = line_view[group][:, block_index, receivers]
        source = jnp.zeros((5, BLOCKS, BLOCK_LINES, EDGE_CELLS), flow_state.dtype)
        source = source.at[:, block_index, receivers].set(jnp.transpose(interp, (2, 0, 1, 3)) - own_rows)
        rhs = residual + source.reshape(fields.shape)
        first = apply_mixer(mixing[3], rhs)
        first = jnp.einsum('vkji,vmk->vmji', first, inverse_z, precision=highest)
        first = apply_mixer(mixing[4], first)
        second = jnp.einsum('vkji,vmj->vkmi', first, inverses[1], precision=highest)
        second = apply_mixer(mixing[5], second)
        final = jnp.einsum('vkji,vmi->vkjm', second, inverses[0], precision=highest)
        return apply_mixer(mixing[6], final)

    return lax.map(one_group, jnp.arange(GROUPS, dtype=jnp.int32))
```

```python
import functools

import jax
import jax.numpy as jnp
from jax import lax
from jax.experimental import pallas as pl
from jax.experimental.pallas import tpu as pltpu
from jax.sharding import PartitionSpec as P

highest = lax.Precision.HIGHEST
f32 = jnp.float32
bf16 = jnp.bfloat16
VARS = 5
SPAN = 4
STRIP = 16
AG_CHUNKS = 4
RS_CHUNKS = 4

in_vmem = pl.BlockSpec(memory_space=pltpu.VMEM)
in_smem = pl.BlockSpec(memory_space=pltpu.SMEM)


def pinned(array):
    return pltpu.with_memory_space_constraint(array, pltpu.VMEM)


def halves(value):
    high = value.astype(bf16)
    return high, (value - high.astype(f32)).astype(bf16)


def beside(*parts):
    return jnp.concatenate(parts, axis=1)


def above(*parts):
    return jnp.concatenate(parts, axis=0)


def product(left, right):
    return jnp.dot(left, right, preferred_element_type=f32)


def rows_product(top, bottom, weights):
    edge = top.shape[1]
    high_top, low_top = halves(top)
    high_bottom, low_bottom = halves(bottom)
    both = product(above(beside(high_top, low_top), beside(high_bottom, low_bottom)), weights)
    return both[:, :edge] + both[:, edge:]


def columns_product(weights, top, bottom):
    edge = top.shape[0]
    high_top, low_top = halves(top)
    high_bottom, low_bottom = halves(bottom)
    both = product(weights, above(beside(high_top, high_bottom), beside(low_top, low_bottom)))
    both = both[:edge] + both[edge:]
    return both[:, :edge], both[:, edge:]


def mixed(coefficients, base, row, values):
    total = coefficients[base + row * VARS] * values[0]
    for column in range(1, VARS):
        total = total + coefficients[base + row * VARS + column] * values[column]
    return total


def expand_kernel(first_group, count, coefficients, signs, fields, along, across, *rest):
    expanded, term_x, term_y = rest[-3:]
    edge = fields.shape[3]

    def pair(step, carry):
        group = step // (SPAN // 2)
        for v in range(VARS):
            top, bottom = fields[v, 2 * step], fields[v, 2 * step + 1]
            term_x[v] = rows_product(top, bottom, along[...])
            left, right = columns_product(across[...], top, bottom)
            term_y[v, :edge] = left
            term_y[v, edge:] = right

        def strip(index, inner):
            plane = index // (edge // STRIP)
            row = lax.rem(index, edge // STRIP) * STRIP
            near = pl.multiple_of(index * STRIP, STRIP)
            slot = 2 * lax.rem(step, SPAN // 2) + plane
            sign = signs[2 * step + plane]
            xs = [term_x[v, pl.ds(near, STRIP), :] for v in range(VARS)]
            ys = [term_y[v, pl.ds(near, STRIP), :] for v in range(VARS)]
            qs = [fields[v, 2 * step + plane, pl.ds(pl.multiple_of(row, STRIP), STRIP), :] for v in range(VARS)]
            for a in range(VARS):
                value = sign * (mixed(coefficients, 0, a, xs) + mixed(coefficients, 25, a, ys))
                expanded[first_group + group, a, pl.ds(row * 8 + slot, STRIP, stride=8), :] = value
                value = -mixed(coefficients, 50, a, qs)
                expanded[first_group + group, a, pl.ds(row * 8 + slot + SPAN, STRIP, stride=8), :] = value
            return inner

        lax.fori_loop(0, 2 * edge // STRIP, strip, 0)
        return carry

    lax.fori_loop(0, count // 2, pair, 0)


def expand(coefficients, signs, fields, along, across, groups, first_group, earlier):
    planes, edge = fields.shape[1], fields.shape[3]
    operands = [coefficients, signs, fields, along, across]
    specs = [in_smem, in_smem, in_vmem, in_vmem, in_vmem]
    aliases = {}
    if earlier is not None:
        operands.append(pinned(earlier))
        specs.append(in_vmem)
        aliases = {5: 0}
    return pl.pallas_call(
        functools.partial(expand_kernel, first_group, planes),
        out_shape=pltpu.VMEM((groups, VARS, edge * 2 * SPAN, edge), f32),
        in_specs=specs,
        out_specs=in_vmem,
        input_output_aliases=aliases,
        scratch_shapes=[pltpu.VMEM((VARS, 2 * edge, edge), f32)] * 2,
        compiler_params=pltpu.CompilerParams(vmem_limit_bytes=20 * 2**20),
        cost_estimate=pl.CostEstimate(
            flops=planes * VARS * 12 * edge**3, bytes_accessed=planes * VARS * 12 * edge**2, transcendentals=0
        ),
        name="expand",
    )(*operands)


def inject_kernel(coefficients, lines, change, held, expanded, mixed_change):
    edge = change.shape[2]
    slots = change.shape[1]

    def strip(index, inner):
        near = pl.ds(pl.multiple_of(index * STRIP, STRIP), STRIP)
        values = [change[v, near, :] for v in range(VARS)]
        for a in range(VARS):
            mixed_change[a, near, :] = mixed(coefficients, 0, a, values)
        return inner

    lax.fori_loop(0, slots // STRIP, strip, 0)

    def receiver(slot, carry):
        line = lines[slot]
        plane = line // edge
        row = lax.rem(line, edge) * (2 * SPAN) + lax.rem(plane, SPAN)
        for a in range(VARS):
            place = (plane // SPAN, a, pl.ds(row, 1), slice(None))
            expanded[place] = expanded[place] + mixed_change[a, pl.ds(slot, 1), :]
        return carry

    lax.fori_loop(0, slots, receiver, 0)


def inject(coefficients, lines, change, expanded):
    return pl.pallas_call(
        inject_kernel,
        out_shape=pltpu.VMEM(expanded.shape, f32),
        in_specs=[in_smem, in_smem, in_vmem, in_vmem],
        out_specs=in_vmem,
        input_output_aliases={3: 0},
        scratch_shapes=[pltpu.VMEM(change.shape, f32)],
        compiler_params=pltpu.CompilerParams(vmem_limit_bytes=20 * 2**20),
        cost_estimate=pl.CostEstimate(flops=change.size * 10, bytes_accessed=change.size * 12, transcendentals=0),
        name="inject",
    )(coefficients, lines, change, pinned(expanded))


def contract_kernel(count, weights, *refs):
    parts, out = refs[:count], refs[count]
    edge = out.shape[2]
    rows = out.shape[1] // edge
    for a in range(VARS):

        def pair(step, carry):
            near = pl.multiple_of(step * 16, 16)
            blocks = [part[g, a, pl.ds(near, 16), :] for part in parts for g in range(part.shape[0])]
            stacked = beside(above(*[block[:8] for block in blocks]), above(*[block[8:] for block in blocks]))
            high, low = halves(stacked)
            both = product(weights[a], above(high, low))
            both = both[:rows] + both[rows:]
            out[a, pl.ds(2 * step, rows, stride=edge), :] = both[:, :edge]
            out[a, pl.ds(2 * step + 1, rows, stride=edge), :] = both[:, edge:]
            return carry

        lax.fori_loop(0, edge // 2, pair, 0, unroll=4)


def contract(weights, parts):
    edge = parts[0].shape[3]
    rows = weights.shape[1] // 2
    return pl.pallas_call(
        functools.partial(contract_kernel, len(parts)),
        out_shape=jax.ShapeDtypeStruct((VARS, rows * edge, edge), f32),
        in_specs=[in_vmem] * (1 + len(parts)),
        out_specs=in_vmem,
        compiler_params=pltpu.CompilerParams(vmem_limit_bytes=24 * 2**20),
        cost_estimate=pl.CostEstimate(
            flops=VARS * edge * edge * weights.shape[1] * weights.shape[2] * 2,
            bytes_accessed=VARS * rows * edge * edge * 4,
            transcendentals=0,
        ),
        name="contract",
    )(weights, *[pinned(part) for part in parts])


def finish_kernel(count, coefficients, across, along, *refs):
    parts, out, first, second = refs[:count], refs[count], refs[count + 1], refs[count + 2]
    edge = out.shape[2]
    start = 2 * edge * pl.program_id(0)

    def mix(base, read, target):
        def strip(index, inner):
            near = pl.ds(pl.multiple_of(index * STRIP, STRIP), STRIP)
            values = [read(v, near) for v in range(VARS)]
            for a in range(VARS):
                target[a, near, :] = mixed(coefficients, base, a, values)
            return inner

        lax.fori_loop(0, 2 * edge // STRIP, strip, 0)

    def gathered(v, near):
        total = parts[0][v, near, :]
        for part in parts[1:]:
            total = total + part[v, near, :]
        return total

    mix(0, gathered, first)
    for v in range(VARS):
        left, right = columns_product(across[v], first[v, :edge], first[v, edge:])
        second[v, :edge] = left
        second[v, edge:] = right
    mix(25, lambda v, near: second[v, near, :], first)
    for v in range(VARS):
        second[v] = rows_product(first[v, :edge], first[v, edge:], along[v])
    mix(50, lambda v, near: second[v, near, :], out)


def finish(coefficients, across, along, parts):
    edge = parts[0].shape[2]
    steps = parts[0].shape[1] // (2 * edge)
    block = pl.BlockSpec((VARS, 2 * edge, edge), lambda step: (0, step, 0))
    return pl.pallas_call(
        functools.partial(finish_kernel, len(parts)),
        out_shape=jax.ShapeDtypeStruct(parts[0].shape, f32),
        grid=(steps,),
        in_specs=[in_smem]
        + [pl.BlockSpec((VARS, 2 * edge, 2 * edge), lambda step: (0, 0, 0))] * 2
        + [block] * len(parts),
        out_specs=block,
        scratch_shapes=[pltpu.VMEM((VARS, 2 * edge, edge), f32)] * 2,
        compiler_params=pltpu.CompilerParams(vmem_limit_bytes=24 * 2**20),
        cost_estimate=pl.CostEstimate(
            flops=steps * VARS * 24 * edge**3, bytes_accessed=parts[0].size * 12, transcendentals=0
        ),
        name="finish",
    )(coefficients, across, along, *parts)


def split(value):
    high = lax.reduce_precision(value, 8, 7)
    return high.astype(bf16), (value - high).astype(bf16)


def right_weights(matrix):
    high, low = split(matrix)
    return jnp.concatenate(
        [jnp.concatenate([high, low], -1), jnp.concatenate([high, jnp.zeros_like(high)], -1)], -2
    )


def left_weights(matrix):
    high, low = split(matrix)
    return jnp.concatenate(
        [jnp.concatenate([high, high], -1), jnp.concatenate([low, jnp.zeros_like(low)], -1)], -2
    )


def chunked(total, wanted, unit):
    while wanted > 1 and total % (wanted * unit):
        wanted -= 1
    return total // wanted


def factors(lines):
    short = max(n for n in range(1, lines + 1) if n * n <= lines and lines % n == 0)
    return short, lines // short


def local(
    zones,
    lines,
    flow_state,
    derivative,
    derivative_z,
    line_inverse,
    line_inverse_z,
    mixers,
    zone_size,
    receiver_line,
    donor_group,
    donor_line,
    stencil_weight,
):
    fields = flow_state[0]
    mixing = mixers[0]
    inverses = line_inverse[0]
    inverse_z = line_inverse_z[0]
    planes, edge = fields.shape[1], fields.shape[3]
    depth = planes * lines
    high_side, wide_side = factors(lines)
    square = high_side == wide_side

    def gather_line(zone, line, step):
        y, x = line // wide_side, line % wide_side
        odd = zone % 2 if square else 0
        shifted = (y + step) % high_side * wide_side + x
        return (1 - odd) * shifted + odd * (y * wide_side + (x + step) % wide_side)

    def scatter_line(zone, line, step):
        y, x = line // wide_side, line % wide_side
        odd = zone % 2 if square else 0
        shifted = y * wide_side + (x + step) % wide_side
        return (1 - odd) * shifted + odd * ((y + step) % high_side * wide_side + x)

    def fetch(value, step):
        pairs = [
            (zone * lines + gather_line(zone, line, step), zone * lines + line)
            for zone in range(zones)
            for line in range(lines)
        ]
        return lax.ppermute(value, ("zone", "line"), pairs)

    def send(value, step):
        pairs = [
            (zone * lines + line, zone * lines + scatter_line(zone, line, step))
            for zone in range(zones)
            for line in range(lines)
        ]
        return lax.ppermute(value, ("zone", "line"), pairs)

    zone, line = lax.axis_index("zone"), lax.axis_index("line")
    sources = [gather_line(zone, line, step) for step in range(high_side)]
    targets = [scatter_line(zone, line, step) for step in range(wide_side)]

    piece = chunked(planes, AG_CHUNKS, SPAN)
    fetched = [
        [fetch(fields[:, at : at + piece], step) for at in range(0, planes, piece)]
        for step in range(1, high_side)
    ]
    receivers = receiver_line[0, 0]
    fetched_receivers = [fetch(receivers, step) for step in range(1, high_side)]

    slots = receiver_line.shape[2]
    capacity = max(2, 5 * slots // (2 * zones))
    line_rows = fields.reshape(VARS, planes * edge, edge)
    wanted = donor_group[0, 0, :, 0]
    member = (wanted[:, None] == jnp.arange(zones, dtype=jnp.int32)[None, :]).astype(jnp.int32)
    position = jnp.sum((jnp.cumsum(member, axis=0) - 1) * member, axis=1)
    slot_index = wanted * capacity + position
    request_rows = jnp.concatenate([donor_line[0, 0].astype(f32), stencil_weight[0, 0][:, None]], axis=1)
    packed = jnp.zeros((zones * capacity, 3), f32).at[slot_index].set(request_rows)
    incoming = lax.all_to_all(
        packed.reshape(zones, capacity, 3), "zone", split_axis=0, concat_axis=0, tiled=True
    )
    first_rows = jnp.take(line_rows, incoming[:, :, 0].astype(jnp.int32), axis=1)
    second_rows = jnp.take(line_rows, incoming[:, :, 1].astype(jnp.int32), axis=1)
    factor = incoming[:, :, 2][None, :, :, None]
    blended = factor * first_rows + (1.0 - factor) * second_rows
    returned = lax.all_to_all(blended, "zone", split_axis=1, concat_axis=1, tiled=True)
    interp = jnp.take(returned.reshape(VARS, zones * capacity, edge), slot_index, axis=1)
    change = interp - jnp.take(line_rows, receivers, axis=1)
    fetched_change = [fetch(change, step) for step in range(1, high_side)]

    merged = jnp.sum(mixing[3][None, :, :, None] * mixing[0:3][:, None, :, :], axis=2).reshape(-1)
    outer = mixing[4:7].reshape(-1)
    inner = mixing[3].reshape(-1)
    along = right_weights(derivative[0].T)
    across = left_weights(derivative[1])
    solve_y = left_weights(inverses[1])
    solve_x = right_weights(jnp.swapaxes(inverses[0], -1, -2))
    active = (jnp.arange(depth, dtype=jnp.int32) < zone_size[0]).astype(f32)
    coupled = jnp.einsum("amk,kn->amn", inverse_z * active[None, None, :], derivative_z, precision=highest)
    table = jnp.stack([inverse_z, coupled])
    table = jnp.concatenate([lax.dynamic_slice_in_dim(table, at * planes, planes, 2) for at in targets], 2)
    table = jnp.concatenate([lax.dynamic_slice_in_dim(table, at * planes, planes, 3) for at in sources], 3)
    count = table.shape[2]
    table = table.reshape(2, VARS, count, -1, SPAN).transpose(1, 2, 3, 0, 4).reshape(VARS, count, -1)
    signs = [-lax.dynamic_slice_in_dim(active, at * planes, planes) for at in sources]

    groups = planes // SPAN
    held = [expand(merged, signs[0], fields, along, across, groups, 0, None)]
    for step in range(1, high_side):
        terms = None
        for index, chunk in enumerate(fetched[step - 1]):
            part = signs[step][index * piece : (index + 1) * piece]
            terms = expand(merged, part, chunk, along, across, groups, index * piece // SPAN, terms)
        held.append(terms)
    held[0] = inject(inner, receivers, change, held[0])
    for step in range(1, high_side):
        held[step] = inject(inner, fetched_receivers[step - 1], fetched_change[step - 1], held[step])

    share = chunked(planes, RS_CHUNKS, 2)
    arrived = []
    for at in range(0, planes, share):
        arrived.append([])
        for step in range(1, wide_side):
            begin = step * planes + at
            arrived[-1].append(send(contract(left_weights(table[:, begin : begin + share]), held), step))
    results = []
    for index, at in enumerate(range(0, planes, share)):
        own = contract(left_weights(table[:, at : at + share]), held)
        result = finish(outer, solve_y, solve_x, [own] + arrived[index])
        results.append(result.reshape(VARS, share, edge, edge))
    return jnp.concatenate(results, axis=1)[None]


def solution(mesh):
    placed = (
        P("zone", None, "line", None, None),
        P(),
        P(),
        P("zone", None, None, None, None),
        P("zone", None, None, None),
        P("zone", None, None, None),
        P("zone"),
        P("zone", "line", None),
        P("zone", "line", None, None),
        P("zone", "line", None, None),
        P("zone", "line", None),
    )
    return jax.shard_map(
        functools.partial(local, mesh.shape["zone"], mesh.shape["line"]),
        mesh=mesh,
        in_specs=placed,
        out_specs=P("zone", None, "line", None, None),
        check_vma=False,
    )
```

```python
import functools
import math

import jax
import jax.numpy as jnp
from jax import lax
from jax.experimental import pallas as pl
from jax.experimental.pallas import tpu as pltpu
from jax.sharding import PartitionSpec as P


f32 = jnp.float32
bf16 = jnp.bfloat16
VARS = 5
SPAN = 4
STRIP = 16
BATCH = 8
UNROLL = 16
FETCHED = (2, 1, 1)
SENT = (2, 2, 2, 1, 1)

in_vmem = pl.BlockSpec(memory_space=pltpu.VMEM)
in_smem = pl.BlockSpec(memory_space=pltpu.SMEM)


def in_hbm(array):
    return pltpu.with_memory_space_constraint(array, pltpu.HBM)


def pinned(array):
    return pltpu.with_memory_space_constraint(array, pltpu.VMEM)


def halves(value):
    high = value.astype(bf16)
    return high, (value - high.astype(f32)).astype(bf16)


def beside(*parts):
    return jnp.concatenate(parts, axis=1)


def above(*parts):
    return jnp.concatenate(parts, axis=0)


def product(left, right):
    return jnp.dot(left, right, preferred_element_type=f32)


def rows_product(top, bottom, weights):
    edge = top.shape[1]
    high_top, low_top = halves(top)
    high_bottom, low_bottom = halves(bottom)
    both = product(above(beside(high_top, low_top), beside(high_bottom, low_bottom)), weights)
    return both[:, :edge] + both[:, edge:]


def columns_product(weights, top, bottom):
    edge = top.shape[0]
    high_top, low_top = halves(top)
    high_bottom, low_bottom = halves(bottom)
    both = product(weights, above(beside(high_top, high_bottom), beside(low_top, low_bottom)))
    both = both[:edge] + both[edge:]
    return both[:, :edge], both[:, edge:]


def mixed(coefficients, base, row, values):
    total = coefficients[0, base, row, 0] * values[0]
    for column in range(1, VARS):
        total = total + coefficients[0, base, row, column] * values[column]
    return total


def mix(coefficients, base, rows, read, target):
    def strip(index, inner):
        near = pl.ds(pl.multiple_of(index * STRIP, STRIP), STRIP)
        values = [read(v, near) for v in range(VARS)]
        for a in range(VARS):
            target[a, near, :] = mixed(coefficients, base, a, values)
        return inner

    lax.fori_loop(0, rows // STRIP, strip, 0)


def expand_group(coefficients, size, first_plane, fields, along, across, expanded, base, term_x, term_y):
    edge = fields.shape[3]

    def pair(step, carry):
        for v in range(VARS):
            top, bottom = fields[v, 2 * step], fields[v, 2 * step + 1]
            term_x[v] = rows_product(top, bottom, along[...])
            left, right = columns_product(across[...], top, bottom)
            term_y[v, :edge] = left
            term_y[v, edge:] = right

        for plane in range(2):
            slot = 2 * step + plane
            sign = jnp.where(first_plane + slot < size, -1.0, 0.0)
            for row in range(0, edge, STRIP):
                near, here = pl.ds(plane * edge + row, STRIP), pl.ds(row, STRIP)
                xs = [term_x[v, near, :] for v in range(VARS)]
                ys = [term_y[v, near, :] for v in range(VARS)]
                qs = [fields[v, slot, here, :] for v in range(VARS)]
                for a in range(VARS):
                    value = sign * (mixed(coefficients, 0, a, xs) + mixed(coefficients, 1, a, ys))
                    expanded[a, pl.ds(base + row * 8 + slot, STRIP, stride=8), :] = value
                    value = mixed(coefficients, 2, a, qs)
                    expanded[a, pl.ds(base + row * 8 + slot + SPAN, STRIP, stride=8), :] = value
        return carry

    lax.fori_loop(0, SPAN // 2, pair, 0)


def expand_kernel(begin, which, coefficients, place, fields, along, across, *rest):
    expanded, term_x, term_y = rest[-3:]
    edge = fields.shape[3]
    offset = begin if expanded.shape[1] > (fields.shape[1] // SPAN) * edge * 2 * SPAN + 8 else 0

    def group(index, carry):
        planes = fields.at[:, pl.ds(index * SPAN, SPAN)]
        first = place[1 + which] + (begin + index) * SPAN
        base = (offset + index) * edge * 2 * SPAN
        expand_group(coefficients, place[0], first, planes, along, across, expanded, base, term_x, term_y)
        return carry

    lax.fori_loop(0, fields.shape[1] // SPAN, group, 0)


def expand(coefficients, place, which, fields, along, across, groups, begin, earlier):
    planes, edge = fields.shape[1], fields.shape[3]
    operands = [coefficients, place, fields, along, across]
    specs = [in_smem, in_smem, in_vmem, in_vmem, in_vmem]
    aliases = {}
    if earlier is not None:
        operands.append(pinned(earlier))
        specs.append(in_vmem)
        aliases = {5: 0}
    return pl.pallas_call(
        functools.partial(expand_kernel, begin, which),
        out_shape=pltpu.VMEM(expanded_shape(groups, edge), f32),
        in_specs=specs,
        out_specs=in_vmem,
        input_output_aliases=aliases,
        scratch_shapes=[pltpu.VMEM((VARS, 2 * edge, edge), f32)] * 2,
        compiler_params=pltpu.CompilerParams(vmem_limit_bytes=8 * 2**20),
        cost_estimate=pl.CostEstimate(
            flops=planes * VARS * 12 * edge**3, bytes_accessed=planes * VARS * 12 * edge**2, transcendentals=0
        ),
        name="expand",
    )(*operands)


def expanded_shape(groups, edge):
    return (VARS, groups * edge * 2 * SPAN + 8, edge)


def rows_of(lines, edge, begin, groups):
    plane = lines // edge
    group = plane // SPAN - begin
    row = (group * edge + lines % edge) * (2 * SPAN) + plane % SPAN
    nowhere = groups * edge * 2 * SPAN + jnp.arange(lines.shape[0], dtype=jnp.int32) % 8
    return jnp.where((group >= 0) & (group < groups), row, nowhere)


def add_change(rows, change, expanded):
    slots = change.shape[1]
    batch = math.gcd(slots, BATCH)

    def receivers(step, carry):
        begin = pl.multiple_of(step * batch, batch)
        places = [(a, pl.ds(rows[begin + index], 1), slice(None)) for index in range(batch) for a in range(VARS)]
        added = [change[a, pl.ds(begin + index, 1), :] for index in range(batch) for a in range(VARS)]
        values = [expanded[place] + value for place, value in zip(places, added)]
        for place, value in zip(places, values):
            expanded[place] = value
        return carry

    lax.fori_loop(0, slots // batch, receivers, 0)


def inject_kernel(rows, change, held, expanded):
    add_change(rows, change, expanded)


def inject(rows, change, expanded):
    return pl.pallas_call(
        inject_kernel,
        out_shape=pltpu.VMEM(expanded.shape, f32),
        in_specs=[in_smem, in_vmem, in_vmem],
        out_specs=in_vmem,
        input_output_aliases={2: 0},
        compiler_params=pltpu.CompilerParams(vmem_limit_bytes=4 * 2**20),
        cost_estimate=pl.CostEstimate(flops=change.size, bytes_accessed=change.size * 12, transcendentals=0),
        name="inject",
    )(rows, change, pinned(expanded))


def close_kernel(begin, which, coefficients, place, rows, fields, along, across, change, expanded, *scratch):
    expand_kernel(begin, which, coefficients, place, fields, along, across, expanded, *scratch)
    add_change(rows, change, expanded)


def close(coefficients, place, which, rows, fields, along, across, change, begin):
    planes, edge = fields.shape[1], fields.shape[3]
    return pl.pallas_call(
        functools.partial(close_kernel, begin, which),
        out_shape=pltpu.VMEM(expanded_shape(planes // SPAN, edge), f32),
        in_specs=[in_smem] * 3 + [in_vmem] * 4,
        out_specs=in_vmem,
        scratch_shapes=[pltpu.VMEM((VARS, 2 * edge, edge), f32)] * 2,
        compiler_params=pltpu.CompilerParams(vmem_limit_bytes=8 * 2**20),
        cost_estimate=pl.CostEstimate(
            flops=planes * VARS * 12 * edge**3, bytes_accessed=planes * VARS * 12 * edge**2, transcendentals=0
        ),
        name="close",
    )(coefficients, place, rows, fields, along, across, change)


def cut_kernel(begin, sizes, fields, *refs):
    outs, arrive = refs[:-1], refs[-1]
    copies = []
    for index, size in enumerate(sizes):
        source = fields.at[:, pl.ds(begin, size)]
        begin += size
        copies.append(pltpu.make_async_copy(source, outs[index], arrive.at[index]))
    for copy in copies:
        copy.start()
    for copy in copies:
        copy.wait()


def cut(fields, begin, sizes, near):
    edge = fields.shape[3]
    shapes = [(VARS, size, edge, edge) for size in sizes]
    return pl.pallas_call(
        functools.partial(cut_kernel, begin, sizes),
        out_shape=[pltpu.VMEM(shape, f32) for shape in shapes],
        in_specs=[in_vmem if near else pl.BlockSpec(memory_space=pl.ANY)],
        out_specs=[in_vmem] * len(shapes),
        scratch_shapes=[pltpu.SemaphoreType.DMA((len(shapes),))],
        compiler_params=pltpu.CompilerParams(vmem_limit_bytes=4 * 2**20),
        name="cut",
    )(fields if near else in_hbm(fields))


def ask_kernel(zones, capacity, place, donors, lines, weights, mixers, *refs):
    requests, receivers, merged, counts, packed = refs[:zones], *refs[zones:]
    slots = donors.shape[0]
    for m in range(3):
        for a in range(VARS):
            for v in range(VARS):
                total = mixers[0, 3, a, 0] * mixers[0, m, 0, v]
                for inner in range(1, VARS):
                    total = total + mixers[0, 3, a, inner] * mixers[0, m, inner, v]
                merged[0, m, a, v] = -total if m == 2 else total

    for step in range(zones):
        counts[step] = step * capacity

    def clear(index, carry):
        for part in range(capacity):
            packed[2, index * capacity + part] = -1.0
            receivers[index * capacity + part] = slots
        return carry

    lax.fori_loop(0, zones, clear, 0)

    def request(index, carry):
        for part in range(2):
            slot = 2 * index + part
            step = donors[slot] - place[0]
            step = jnp.where(step < 0, step + zones, step)
            entry = counts[step]
            counts[step] = entry + 1
            packed[0, entry] = lines[0, slot]
            packed[1, entry] = lines[1, slot]
            packed[2, entry] = weights[slot]
            receivers[entry] = slot
        return carry

    lax.fori_loop(0, slots // 2, request, 0)
    for step in range(zones):

        def hand(index, carry):
            for part in range(math.gcd(capacity, BATCH)):
                entry = index * math.gcd(capacity, BATCH) + part
                for kind in range(3):
                    requests[step][kind, entry] = packed[kind, step * capacity + entry]
            return carry

        lax.fori_loop(0, capacity // math.gcd(capacity, BATCH), hand, 0)


def ask(zones, capacity, place, donors, lines, weights, mixers):
    out = pl.pallas_call(
        functools.partial(ask_kernel, zones, capacity),
        out_shape=[jax.ShapeDtypeStruct((3, capacity), f32)] * zones
        + [
            jax.ShapeDtypeStruct((zones * capacity,), jnp.int32),
            jax.ShapeDtypeStruct((1, 3, VARS, VARS), f32),
        ],
        in_specs=[in_smem] * 5,
        out_specs=[in_smem] * (zones + 2),
        scratch_shapes=[pltpu.SMEM((zones,), jnp.int32), pltpu.SMEM((3, zones * capacity), f32)],
        compiler_params=pltpu.CompilerParams(vmem_limit_bytes=4 * 2**20),
        name="ask",
    )(place, donors, lines, weights, mixers)
    return list(out[:-2]), out[-2], out[-1]


def prepare_kernel(planes, counts, place, derivative, derivative_z, inverses, inverse_z, *refs):
    along, across, solve_y, solve_x, staying = refs[:5]
    leaving = refs[5:]
    sources, targets = counts
    edge, depth = derivative.shape[1], derivative_z.shape[0]
    def right(out, matrix):
        high, low = halves(matrix)
        out[:edge, :edge] = high
        out[:edge, edge:] = low
        out[edge:, :edge] = high
        out[edge:, edge:] = jnp.zeros_like(low)

    def left(out, matrix):
        high, low = halves(matrix)
        out[:edge, :edge] = high
        out[:edge, edge:] = high
        out[edge:, :edge] = low
        out[edge:, edge:] = jnp.zeros_like(low)

    right(along, derivative[0].T)
    left(across, derivative[1])
    for v in range(VARS):
        right(solve_x.at[v], inverses[0, 0, v].T)
        left(solve_y.at[v], inverses[0, 1, v])

    columns = 2 * planes * sources

    def pattern(kind, repeats):
        at = lax.broadcasted_iota(jnp.int32, (depth, 2 * columns), 0)
        column = lax.broadcasted_iota(jnp.int32, (depth, 2 * columns), 1)
        inside = lax.rem(column, columns)
        source = inside // (2 * planes)
        first = place[1]
        for index in range(1, sources):
            first = jnp.where(source == index, place[1 + index], first)
        within = lax.rem(inside, 2 * planes)
        plane = first + within // (2 * SPAN) * SPAN + lax.rem(within, SPAN)
        wanted = (at == plane) & (lax.rem(within, 2 * SPAN) // SPAN == kind) & (column < repeats * columns)
        return jnp.where(wanted, 1.0, 0.0).astype(bf16)

    def picked(first):
        at = lax.broadcasted_iota(jnp.int32, (-(-planes // 8) * 8, depth), 0)
        column = lax.broadcasted_iota(jnp.int32, (-(-planes // 8) * 8, depth), 1)
        return jnp.where((at < planes) & (column - first == at), 1.0, 0.0)

    sets = [picked(place[1 + sources + step]) for step in range(1, targets)] + [picked(place[1])]
    chosen = jnp.concatenate(sets, axis=0).astype(bf16)
    plain_high, coupled_high = pattern(0, 2), pattern(1, 2)
    plain_low, coupled_low = pattern(0, 1), pattern(1, 1)
    active = lax.broadcasted_iota(jnp.int32, (depth, depth), 1) < place[0]
    z_high, z_low = halves(derivative_z[...])
    for a in range(VARS):
        solve = inverse_z[0, a]
        high, low = halves(solve)
        cut_high, cut_low = halves(jnp.where(active, solve, 0.0))
        coupled = product(cut_high, z_high) + (product(cut_high, z_low) + product(cut_low, z_high))
        both_high, both_low = halves(coupled)
        top = (product(high, plain_high) + product(both_high, coupled_high)).astype(bf16)
        bottom = (product(low, plain_low) + product(both_low, coupled_low)).astype(bf16)
        top, bottom = product(chosen, top), product(chosen, bottom)
        begin = 0
        for out in list(leaving) + [staying]:
            rows = out.shape[1] // 2
            out[a] = above(top[begin : begin + rows], bottom[begin : begin + rows]).astype(bf16)
            begin += rows


def prepare(place, derivative, derivative_z, line_inverse, line_inverse_z, planes, sources, targets):
    edge = derivative.shape[1]
    square = jax.ShapeDtypeStruct((2 * edge, 2 * edge), bf16)
    squares = jax.ShapeDtypeStruct((VARS, 2 * edge, 2 * edge), bf16)
    table = jax.ShapeDtypeStruct((VARS, 2 * (-(-planes // 8) * 8), 4 * planes * sources), bf16)
    out = pl.pallas_call(
        functools.partial(prepare_kernel, planes, (sources, targets)),
        out_shape=[square, square, squares, squares] + [table] * targets,
        in_specs=[in_smem] + [in_vmem] * 4,
        out_specs=[in_vmem] * (4 + targets),
        compiler_params=pltpu.CompilerParams(vmem_limit_bytes=12 * 2**20),
        name="prepare",
    )(place, derivative, derivative_z, line_inverse, line_inverse_z)
    return out[:5], out[5:]


def blend_kernel(zones, receivers, fields, *refs):
    requests, blended, own = refs[:zones], refs[zones : 2 * zones], refs[2 * zones]
    capacity = blended[0].shape[1]
    batch = math.gcd(capacity, BATCH)
    slots = own.shape[1]
    several = math.gcd(slots, BATCH)

    for request, out in zip(requests, blended):

        def block(step, carry):
            @pl.when(request[2, step * batch] >= 0)
            def _():
                for index in range(batch):
                    slot = step * batch + index
                    weight = request[2, slot]
                    live = weight >= 0
                    first = jnp.where(live, request[0, slot], 0.0).astype(jnp.int32)
                    second = jnp.where(live, request[1, slot], 0.0).astype(jnp.int32)
                    for v in range(VARS):
                        near = fields[v, pl.ds(first, 1), :]
                        far = fields[v, pl.ds(second, 1), :]
                        out[v, pl.ds(slot, 1), :] = weight * near + (1.0 - weight) * far

            return carry

        lax.fori_loop(0, capacity // batch, block, 0)

    def keep(step, carry):
        for index in range(several):
            slot = step * several + index
            line = receivers[slot]
            for v in range(VARS):
                own[v, pl.ds(slot, 1), :] = fields[v, pl.ds(line, 1), :]
        return carry

    lax.fori_loop(0, slots // several, keep, 0)


def blend(requests, receivers, fields, capacity):
    edge, slots, zones = fields.shape[2], receivers.shape[0], len(requests)
    out = pl.pallas_call(
        functools.partial(blend_kernel, zones),
        out_shape=[jax.ShapeDtypeStruct((VARS, capacity, edge), f32)] * zones
        + [jax.ShapeDtypeStruct((VARS, slots, edge), f32)],
        in_specs=[in_smem, in_vmem] + [in_smem] * zones,
        out_specs=[in_vmem] * (zones + 1),
        compiler_params=pltpu.CompilerParams(vmem_limit_bytes=8 * 2**20),
        cost_estimate=pl.CostEstimate(
            flops=zones * VARS * capacity * edge * 3,
            bytes_accessed=zones * VARS * capacity * edge * 12,
            transcendentals=0,
        ),
        name="blend",
    )(receivers, fields, *requests)
    return list(out[:-1]), out[-1]


def pick_kernel(zones, coefficients, receivers, own, *refs):
    returned, change, raw = refs[:zones], refs[zones], refs[zones + 1]
    slots = change.shape[1]
    capacity = returned[0].shape[1]
    batch = math.gcd(capacity, BATCH)

    for step, rows in enumerate(returned):

        def block(index, carry):
            @pl.when(receivers[step * capacity + index * batch] < slots)
            def _():
                for entry in range(batch):
                    slot = receivers[step * capacity + index * batch + entry]
                    for v in range(VARS):
                        raw[v, pl.ds(slot, 1), :] = rows[v, pl.ds(index * batch + entry, 1), :]

            return carry

        lax.fori_loop(0, capacity // batch, block, 0)
    mix(coefficients, 3, slots, lambda v, near: raw[v, near, :] - own[v, near, :], change)


def pick(coefficients, receivers, returned, own):
    slots, edge = own.shape[1:]
    return pl.pallas_call(
        functools.partial(pick_kernel, len(returned)),
        out_shape=jax.ShapeDtypeStruct(own.shape, f32),
        in_specs=[in_smem] * 2 + [in_vmem] * (1 + len(returned)),
        out_specs=in_vmem,
        scratch_shapes=[pltpu.VMEM((VARS, slots + 8, edge), f32)],
        compiler_params=pltpu.CompilerParams(vmem_limit_bytes=8 * 2**20),
        cost_estimate=pl.CostEstimate(flops=own.size * 10, bytes_accessed=own.size * 12, transcendentals=0),
        name="pick",
    )(coefficients, receivers, own, *returned)


def contract_kernel(count, shares, weights, *refs):
    parts, outs = refs[:count], refs[count : count + len(shares)]
    buffer, leave = refs[-2:]
    edge = parts[0].shape[2]
    slots = weights.shape[1] // 2
    planes = sum(shares)
    unroll = min(UNROLL, edge // 2)

    def copies(a, side):
        begin, out_of = 0, []
        for index, (share, out) in enumerate(zip(shares, outs)):
            rows = buffer.at[side, pl.ds(begin * edge, share * edge)]
            out_of.append(pltpu.make_async_copy(rows, out.at[a], leave.at[side, index]))
            begin += share
        return out_of

    def variable(a, carry):
        side = lax.rem(a, 2)

        @pl.when(a >= 2)
        def _():
            for copy in copies(a - 2, side):
                copy.wait()

        def pairs(step, inner):
            for index in range(unroll):
                j = 2 * (step * unroll + index)
                near = pl.multiple_of(j * 8, 16)
                blocks = [
                    part[a, pl.ds(near + group * edge * 2 * SPAN, 16), :]
                    for part in parts
                    for group in range(part.shape[1] // (edge * 2 * SPAN))
                ]
                stacked = beside(above(*[block[:8] for block in blocks]), above(*[block[8:] for block in blocks]))
                high, low = halves(stacked)
                both = product(weights[a], above(high, low))
                both = both[:slots] + both[slots:]
                buffer[side, pl.ds(j, planes, stride=edge), :] = both[:planes, :edge]
                buffer[side, pl.ds(j + 1, planes, stride=edge), :] = both[:planes, edge:]
            return inner

        lax.fori_loop(0, edge // (2 * unroll), pairs, 0)
        for copy in copies(a, side):
            copy.start()
        return carry

    lax.fori_loop(0, VARS, variable, 0)
    for a in range(VARS - 2, VARS):
        for copy in copies(a, a % 2):
            copy.wait()


def contract(weights, shares, parts):
    edge = parts[0].shape[2]
    return pl.pallas_call(
        functools.partial(contract_kernel, len(parts), shares),
        out_shape=[jax.ShapeDtypeStruct((VARS, share * edge, edge), f32) for share in shares],
        in_specs=[in_vmem] * (1 + len(parts)),
        out_specs=[pl.BlockSpec(memory_space=pl.ANY)] * len(shares),
        scratch_shapes=[
            pltpu.VMEM((2, sum(shares) * edge, edge), f32),
            pltpu.SemaphoreType.DMA((2, len(shares))),
        ],
        compiler_params=pltpu.CompilerParams(vmem_limit_bytes=8 * 2**20),
        cost_estimate=pl.CostEstimate(
            flops=VARS * edge * edge * weights.shape[1] * weights.shape[2] * 2,
            bytes_accessed=VARS * sum(shares) * edge * edge * 4,
            transcendentals=0,
        ),
        name="contract",
    )(weights, *[pinned(part) for part in parts])


def finish_kernel(count, coefficients, across, along, *refs):
    parts, (out, first, second) = refs[:count], refs[-3:]
    edge = out.shape[2]

    def gathered(v, near):
        total = parts[0][v, near, :]
        for part in parts[1:]:
            total = total + part[v, near, :]
        return total

    mix(coefficients, 4, 2 * edge, gathered, first)
    for v in range(VARS):
        left, right = columns_product(across[v], first[v, :edge], first[v, edge:])
        second[v, :edge] = left
        second[v, edge:] = right
    mix(coefficients, 5, 2 * edge, lambda v, near: second[v, near, :], first)
    for v in range(VARS):
        second[v] = rows_product(first[v, :edge], first[v, edge:], along[v])
    mix(coefficients, 6, 2 * edge, lambda v, near: second[v, near, :], out)


def finish(coefficients, across, along, own, arrived, begin, earlier):
    edge = own.shape[2]
    steps = arrived[0].shape[1] // (2 * edge)
    here = pl.BlockSpec((VARS, 2 * edge, edge), lambda step: (0, step, 0))
    there = pl.BlockSpec((VARS, 2 * edge, edge), lambda step: (0, step + begin // 2, 0))
    operands = [coefficients, across, along, own] + arrived
    specs = [in_smem] + [pl.BlockSpec((VARS, 2 * edge, 2 * edge), lambda step: (0, 0, 0))] * 2
    specs += [there] + [here] * len(arrived)
    aliases = {}
    if earlier is not None:
        aliases = {len(operands): 0}
        operands.append(earlier)
        specs.append(pl.BlockSpec(memory_space=pl.ANY))
    return pl.pallas_call(
        functools.partial(finish_kernel, 1 + len(arrived)),
        out_shape=jax.ShapeDtypeStruct(own.shape, f32),
        grid=(steps,),
        in_specs=specs,
        out_specs=there,
        input_output_aliases=aliases,
        scratch_shapes=[pltpu.VMEM((VARS, 2 * edge, edge), f32)] * 2,
        compiler_params=pltpu.CompilerParams(vmem_limit_bytes=20 * 2**20),
        cost_estimate=pl.CostEstimate(
            flops=steps * VARS * 24 * edge**3, bytes_accessed=arrived[0].size * 12, transcendentals=0
        ),
        name="finish",
    )(*operands)


def divided(total, pieces, unit):
    whole = sum(pieces)
    if all(total * piece % (whole * unit) == 0 for piece in pieces):
        return [total * piece // whole for piece in pieces]
    return [total]


def factors(lines):
    short = max(n for n in range(1, lines + 1) if n * n <= lines and lines % n == 0)
    return short, lines // short


def local(
    zones,
    lines,
    flow_state,
    derivative,
    derivative_z,
    line_inverse,
    line_inverse_z,
    mixers,
    zone_size,
    receiver_line,
    donor_group,
    donor_line,
    stencil_weight,
):
    fields = flow_state[0]
    planes, edge = fields.shape[1], fields.shape[3]
    high_side, wide_side = factors(lines)
    square = high_side == wide_side

    def gather_line(zone, line, step):
        y, x = line // wide_side, line % wide_side
        odd = zone % 2 if square else 0
        shifted = (y + step) % high_side * wide_side + x
        return (1 - odd) * shifted + odd * (y * wide_side + (x + step) % wide_side)

    def scatter_line(zone, line, step):
        y, x = line // wide_side, line % wide_side
        odd = zone % 2 if square else 0
        shifted = y * wide_side + (x + step) % wide_side
        return (1 - odd) * shifted + odd * ((y + step) % high_side * wide_side + x)

    def fetch(value, step):
        pairs = [
            (zone * lines + gather_line(zone, line, step), zone * lines + line)
            for zone in range(zones)
            for line in range(lines)
        ]
        return lax.ppermute(value, ("zone", "line"), pairs)

    def send(value, step):
        pairs = [
            (zone * lines + line, zone * lines + scatter_line(zone, line, step))
            for zone in range(zones)
            for line in range(lines)
        ]
        return lax.ppermute(value, ("zone", "line"), pairs)

    zone, line = lax.axis_index("zone"), lax.axis_index("line")
    sources = [gather_line(zone, line, step) for step in range(high_side)]
    targets = [scatter_line(zone, line, step) for step in range(wide_side)]

    pieces = divided(planes, FETCHED, SPAN)
    receivers = receiver_line[0, 0]
    first_planes = [zone_size[0]] + [at * planes for at in sources + targets]
    place = jnp.stack(first_planes).astype(jnp.int32)
    (chunk,) = cut(fields, 0, pieces[:1], False)
    with jax.named_scope("first"):
        fetched = [[fetch(chunk, step)] for step in range(1, high_side)]
    fetched_receivers = [fetch(receivers, step) for step in range(1, high_side)]

    slots = receiver_line.shape[2]
    capacity = max(2, 5 * slots // (2 * zones))
    pairs = jnp.swapaxes(donor_line[0, 0], 0, 1).astype(f32)
    donors, pairs, weights, chunk = lax.optimization_barrier(
        (donor_group.reshape(-1), pairs, stencil_weight.reshape(-1), chunk)
    )
    here = jnp.reshape(zone, (1,)).astype(jnp.int32)
    requests, receiver_slots, merged = ask(zones, capacity, here, donors, pairs, weights, mixers)

    def turn(value, step):
        there = [
            (at * lines + place, (at + step) % zones * lines + place) for at in range(zones) for place in range(lines)
        ]
        return lax.ppermute(value, ("zone", "line"), there)

    with jax.named_scope("request"):
        requests = requests[:1] + [turn(requests[step], step) for step in range(1, zones)]
    if len(pieces) > 1:
        rest = cut(fields, pieces[0], pieces[1:], True)
        for step in range(1, high_side):
            fetched[step - 1] += [fetch(chunk, step) for chunk in rest]

    shares = divided(planes, SENT, 2)
    operators, leaving = prepare(
        place, derivative, derivative_z, line_inverse, line_inverse_z, planes, high_side, wide_side
    )
    along, across, solve_y, solve_x, staying = operators

    blended, own_rows = blend(requests, receivers, fields.reshape(VARS, planes * edge, edge), capacity)
    with jax.named_scope("answer"):
        returned = blended[:1] + [turn(blended[step], zones - step) for step in range(1, zones)]

    source, own_rows = lax.optimization_barrier((fields, own_rows))
    kept = expand(merged, place, 0, source, along, across, planes // SPAN, 0, None)
    before = planes - pieces[-1]
    early = []
    for step in range(1, high_side if before else 1):
        early.append(expand(merged, place, step, fetched[step - 1][0], along, across, before // SPAN, 0, None))
    returned, kept, early = lax.optimization_barrier((returned, kept, early))
    change = pick(mixers, receiver_slots, returned, own_rows)
    fetched_change = [fetch(change, step) for step in range(1, high_side)]
    change, fetched_receivers = lax.optimization_barrier((change, fetched_receivers))
    held = [inject(rows_of(receivers, edge, 0, planes // SPAN), change, kept)]
    for step in range(1, high_side):
        lines_there, change_there = fetched_receivers[step - 1], fetched_change[step - 1]
        if before:
            terms, begin = early[step - 1], pieces[0]
            for piece, chunk in zip(pieces[1:-1], fetched[step - 1][1:-1]):
                terms = expand(merged, place, step, chunk, along, across, before // SPAN, begin // SPAN, terms)
                begin += piece
            held.append(inject(rows_of(lines_there, edge, 0, before // SPAN), change_there, terms))
        rows = rows_of(lines_there, edge, before // SPAN, pieces[-1] // SPAN)
        last = fetched[step - 1][-1]
        held.append(close(merged, place, step, rows, last, along, across, change_there, before // SPAN))

    arrived = []
    for step in range(1, wide_side):
        partial = contract(leaving[step - 1], shares, held)
        arrived.append([send(part, step) for part in partial])
    (own,) = contract(staying, [planes], held)
    result, begin = None, 0
    for index, share in enumerate(shares):
        chunk = [parts[index] for parts in arrived]
        result = finish(mixers, solve_y, solve_x, own, chunk, begin, result)
        begin += share
    return result.reshape(flow_state.shape)


def solution(mesh):
    placed = (
        P("zone", None, "line", None, None),
        P(),
        P(),
        P("zone", None, None, None, None),
        P("zone", None, None, None),
        P("zone", None, None, None),
        P("zone"),
        P("zone", "line", None),
        P("zone", "line", None, None),
        P("zone", "line", None, None),
        P("zone", "line", None),
    )
    return jax.shard_map(
        functools.partial(local, mesh.shape["zone"], mesh.shape["line"]),
        mesh=mesh,
        in_specs=placed,
        out_specs=P("zone", None, "line", None, None),
        check_vma=False,
    )
```
